32 devices in a mesh: micro: 4 (over z), grid: 8 (over y, x, core).
Axes of the slice: x: 2, y: 2, z: 4, core: 2. Of those that a mesh axis runs over, the one named last changes fastest.
Arguments:
- orbitals: float32 [2, 32, 64, 16, 256], P(None, 'micro', None, 'grid'), may hold values from -14 to 14
- local_potential: float32 [32, 16, 256], P('micro', 'grid'), may hold values from -1 to 1
- projectors: float32 [2, 32, 16, 256], P(None, None, 'grid'), may hold values from -0.09375 to 0.09375
- strengths: float32 [2, 32], replicated, may hold values from 1 to 12
- material: int32 [32], replicated, may hold values from 0 to 1
- proj_kind: int32 [32], replicated, may hold values from 0 to 1
- point_cell: int32 [32], replicated, may hold values from 0 to 1999
- vector_now: float32 [2000], replicated, may hold values from -3 to 3
- vector_old: float32 [2000], replicated, may hold values from -3 to 3
Outputs:
- orbitals_out: float32 [2, 32, 64, 16, 256], P(None, 'micro', None, 'grid')
- vector_field: float32 [2000], replicated
The draws below stay inside these ranges and needn't reach their ends.
All inputs are finite; a program needn't handle non-finite values.
Results may differ from the reference program's by a relative error of at most 0.0003.
Values sent between devices are 32-bit elements; how exact they have to be, the bound alone decides.
A program may use at most 128 MiB of HBM per device.

```python
import math
import jax
import jax.numpy as jnp
from jax import lax

NX = 16
NY = 16
NZ = 16
ORB = 64
NPROJ = 32
KINDS = 2
POINTS = 32
MACRO_CELLS = 2000
STEPS = 2
ORDER = 4


def draw_orbitals(key, part):
    subkeys = jax.random.split(key, 3)
    cells = NY * NZ
    z_index = (jnp.arange(cells, dtype=jnp.int32) % NZ).astype(jnp.float32)
    wave_modes = jax.random.randint(subkeys[0], (POINTS, ORB, 1, 1), 1, NZ // 4 + 1).astype(jnp.float32)
    phases = jax.random.uniform(subkeys[1], (POINTS, ORB, 1, 1), minval=-math.pi, maxval=math.pi)
    angular_offset = 2.0 * math.pi * wave_modes * z_index / NZ + phases
    planes = jnp.arange(NX).astype(jnp.float32)
    growing_amplitude = (3.0 ** (planes / (NX - 1))).reshape(1, 1, NX, 1)
    large_scale_share = 0.6 * jnp.clip(jax.random.normal(subkeys[2], (2, POINTS, ORB, NX, cells)), -6.0, 6.0)
    scaling_coefficient = jnp.ones((POINTS, ORB, 1, 1), jnp.float32)
    oscillating_cosine = jnp.stack([jnp.cos(angular_offset), jnp.sin(angular_offset)])
    return (growing_amplitude * scaling_coefficient * (oscillating_cosine + large_scale_share)).astype(jnp.float32)


def with_ends(drawn, stream_key, low, top_value):
    shape = drawn.shape
    index_at = [jax.random.randint(jax.random.fold_in(stream_key, axis), (), 0, shape[axis]) for axis in range(len(shape))]
    drawn = drawn.at[tuple(index_at)].set(low)
    longest = shape.index(max(shape))
    index_at[longest] = (index_at[longest] + 1) % shape[longest]
    return drawn.at[tuple(index_at)].set(top_value)


def block_levels(stream_key, shape, cuts, low, largest):
    def one(dim, parts):
        steps = jax.random.uniform(jax.random.fold_in(jax.random.fold_in(stream_key, 6), dim), (parts,), jnp.float32, low / len(cuts), largest / len(cuts))
        return jnp.repeat(jnp.exp(steps), shape[dim] // parts).reshape((-1,) + (1,) * (len(shape) - dim - 1))

    gain = one(*cuts[0])
    for cut in cuts[1:]:
        gain = gain * one(*cut)
    return gain


def noise(stream_key, shape, width, reach, pieces=(), kind=jnp.bfloat16):
    values = jax.random.normal(stream_key, shape, jnp.float32) * width
    if len(pieces) > 0:
        values = block_levels(stream_key, shape, pieces, -0.22, 0.18) * values
    return jnp.clip(values, min=-reach, max=reach).astype(kind)


def setup_inputs(seed: int = 0) -> dict:
    keys = jax.random.split(jax.random.key(seed), 10)
    return {
        "orbitals": draw_orbitals(jax.random.fold_in(keys[9], 71), 0),
        "local_potential": jnp.clip(jax.random.uniform(keys[1], (POINTS, NX, NY * NZ), jnp.float32, -1.0, 1.0) * block_levels(keys[1], (POINTS, NX, NY * NZ), ((0, 4), (1, 8)), -0.4, 0.0), -1.0, 1.0),
        "projectors": noise(keys[2], (KINDS, NPROJ, NX, NY * NZ), (NX * NY * NZ) ** -0.5, 0.09375, ((2, 8),), jnp.float32),
        "strengths": jnp.clip(jnp.exp(jax.random.uniform(keys[3], (KINDS, NPROJ), jnp.float32, math.log(1.0), math.log(12.0))), 1.0, 12.0),
        "material": with_ends(jax.random.randint(keys[4], (POINTS,), 0, 2), jax.random.fold_in(keys[4], 1), 0, 1).astype(jnp.int32),
        "proj_kind": with_ends(jax.random.randint(keys[5], (POINTS,), 0, KINDS), jax.random.fold_in(keys[5], 1), 0, KINDS - 1).astype(jnp.int32),
        "point_cell": with_ends(jax.random.randint(keys[6], (POINTS,), 0, MACRO_CELLS), jax.random.fold_in(keys[6], 1), 0, MACRO_CELLS - 1).astype(jnp.int32),
        "vector_now": noise(keys[7], (MACRO_CELLS,), 0.5, 3.0, (), jnp.float32),
        "vector_old": noise(keys[8], (MACRO_CELLS,), 0.5, 3.0, (), jnp.float32),
    }


SPACING = 0.64
TIME_STEP = 0.05
COURANT = 0.9
COUPLING = 1.0
HIGHEST = lax.Precision.HIGHEST


def z_gradient(field):
    extent = field.shape
    blocks = field.reshape(extent[:-1] + (NY, NZ))
    change = jnp.roll(blocks, -1, len(extent)) - jnp.roll(blocks, 1, len(extent))
    return change.reshape(extent) / (2.0 * SPACING)


def neighbour_sums(field):
    extent = field.shape
    blocks = field.reshape(extent[:-1] + (NY, NZ))
    horizontal_direction = jnp.roll(blocks, 1, 3) + jnp.roll(blocks, -1, 3)
    along_y = jnp.roll(blocks, 1, 4) + jnp.roll(blocks, -1, 4)
    forward = jnp.roll(blocks, -1, 5)
    backward = jnp.roll(blocks, 1, 5)
    beside_all = (horizontal_direction + along_y + forward + backward).reshape(extent)
    field_gradient = (forward - backward).reshape(extent) / (2.0 * SPACING)
    return beside_all, field_gradient


def apply_hamiltonian(field, field_at, potential, beta_flat, weights):
    beside_all, field_gradient = neighbour_sums(field)
    diagonal = 3.0 / SPACING ** 2 + 0.5 * field_at * field_at + potential
    kinetic = diagonal * field - beside_all / (2.0 * SPACING ** 2)
    drift = jnp.stack([field_gradient[1], -field_gradient[0]]) * field_at
    flattened_rows = field.reshape(-1, beta_flat.shape[1])
    intersection = jnp.dot(flattened_rows, beta_flat.T, precision=HIGHEST)
    intersection = intersection.reshape(field.shape[:3] + (-1,)) * weights[None, :, None, :]
    nonlocal_part = jnp.dot(intersection.reshape(flattened_rows.shape[0], -1), beta_flat, precision=HIGHEST)
    return kinetic + drift + nonlocal_part.reshape(field.shape)


def point_current(field, field_at, occupied):
    field_gradient = z_gradient(field)
    flow = field[0] * field_gradient[1] - field[1] * field_gradient[0]
    density = field[0] * field[0] + field[1] * field[1]
    per_orbital = jnp.sum(flow + field_at * density, axis=(2, 3))
    return jnp.sum(per_orbital * occupied, axis=1) * (2.0 / (ORB * NX * NY * NZ))


def reference(orbitals, local_potential, projectors, strengths, material, proj_kind, point_cell, vector_now, vector_old):
    beta_flat = projectors.reshape(KINDS * NPROJ, NX * NY * NZ)
    kind_onehot = (proj_kind[:, None] == jnp.arange(KINDS, dtype=jnp.int32)[None, :]).astype(jnp.float32)
    weights = (kind_onehot[:, :, None] * strengths[None]).reshape(POINTS, KINDS * NPROJ)
    orbital_ids = jnp.arange(ORB, dtype=jnp.int32)
    occupied = ((orbital_ids[None, :] < ORB // 2) | (material[:, None] == 1)).astype(jnp.float32)
    potential = local_potential[:, None]
    macro_ids = jnp.arange(MACRO_CELLS, dtype=jnp.int32)
    placement = (point_cell[:, None] == macro_ids[None, :]).astype(jnp.float32)
    field = orbitals
    present = vector_now
    previous = vector_old
    for step_index in range(STEPS):
        field_at = present[point_cell].reshape(POINTS, 1, 1, 1)
        summed = field
        taylor_term = field
        for degree in range(1, ORDER + 1):
            applied = apply_hamiltonian(taylor_term, field_at, potential, beta_flat, weights)
            taylor_term = (TIME_STEP / degree) * jnp.stack([applied[1], -applied[0]])
            summed = summed + taylor_term
        field = summed
        currents = point_current(field, field_at, occupied)
        accumulate_current = jnp.dot(currents, placement, precision=HIGHEST)
        extended_with_zeros = jnp.pad(present, 1)
        curvature = extended_with_zeros[2:] + extended_with_zeros[:-2] - 2.0 * present
        following = 2.0 * present - previous + COURANT ** 2 * curvature - COUPLING * accumulate_current
        previous = present
        present = following
    return field * occupied[None, :, :, None, None], present
```

```python
import functools

import jax
import jax.numpy as jnp
from jax import lax
from jax.experimental import pallas as pl
from jax.experimental.pallas import tpu as pltpu
from jax.sharding import PartitionSpec as P

NZ = 16
STEPS = 2
ORDER = 4

SPACING = 0.64
TIME_STEP = 0.05
COURANT = 0.9
COUPLING = 1.0
HIGHEST = lax.Precision.HIGHEST
F32 = jnp.float32
BF16 = jnp.bfloat16


def split(value):
    high = value.astype(BF16)
    low = (value - high.astype(F32)).astype(BF16)
    return jnp.concatenate([high, low], axis=-1)


def stencil_matrix(cells):
    row = lax.broadcasted_iota(jnp.int32, (cells, cells), 0)
    col = lax.broadcasted_iota(jnp.int32, (cells, cells), 1)
    z = col % NZ
    forward = row == (col - z + (z + 1) % NZ)
    backward = row == (col - z + (z + NZ - 1) % NZ)
    y_next = row == (col + NZ) % cells
    y_last = row == (col + cells - NZ) % cells
    one = lambda m: m.astype(F32)
    beside = one(forward) + one(backward) + one(y_next) + one(y_last)
    both = jnp.concatenate([beside, one(forward) - one(backward)], axis=1)
    return jnp.concatenate([both, both], axis=0).astype(BF16)


def nt_dot(left, right):
    return lax.dot_general(left, right, (((1,), (1,)), ((), ())), preferred_element_type=F32)


def step_kernel(
    rows, norm, last, scal_ref, limit_ref, field_ref, side_ref, weight_ref, stencil_ref, mix_ref,
    out_ref, current_ref,
    term_a, term_b, total_ref, parts_ref, back_ref, fore_ref, diag_ref,
):
    planes, cells = total_ref.shape[0], total_ref.shape[2]
    half = rows // 2
    nproj = mix_ref.shape[0] // 4
    a = scal_ref[0]
    k2 = 1.0 / (2.0 * SPACING**2)

    def setup(x, overlap):
        beta = side_ref[x, :nproj, :]
        high = beta.astype(BF16).astype(F32)
        low = beta - high
        zero = jnp.zeros_like(high)
        back_ref[x] = jnp.concatenate([high, high, low, zero], axis=0).astype(BF16)
        fore = jnp.concatenate([high, low, zero, zero], axis=0).astype(BF16)
        fore_ref[x] = jnp.concatenate([fore, fore], axis=1)
        diag_ref[x] = jnp.broadcast_to(
            side_ref[x, nproj:nproj + 1, :] + (3.0 / SPACING**2 + 0.5 * a * a), (8, cells)
        )
        value = field_ref[x, :rows, :]
        total_ref[x] = value
        pieces = split(value)
        parts_ref[x] = pieces
        return overlap + nt_dot(pieces, fore_ref[x])

    overlap = lax.fori_loop(0, planes, setup, jnp.zeros((rows, 4 * nproj), F32))
    lane = lax.broadcasted_iota(jnp.int32, (rows, 4 * nproj), 1)
    middle = (lane >= nproj) & (lane < 2 * nproj)
    slots = (total_ref, term_a, term_b)
    source = total_ref
    for degree in range(1, ORDER + 1):
        target = term_a if degree % 2 == 1 else term_b
        scale = TIME_STEP / degree
        c = jnp.dot(overlap, mix_ref[...], precision=HIGHEST, preferred_element_type=F32) * weight_ref[0:1, :]
        high = c.astype(BF16).astype(F32)
        coefficients = jnp.where(middle, c - high, high).astype(BF16)
        if degree == 1:
            read = lambda x: field_ref[x, :rows, :]
        else:
            read = functools.partial(lambda ref, x: ref[x], source)

        def body(x, overlap, read=read, target=target, scale=scale, coefficients=coefficients, degree=degree):
            up = lax.rem(x + 1, planes)
            down = lax.rem(x + planes - 1, planes)
            both = jnp.dot(parts_ref[x], stencil_ref[...], preferred_element_type=F32)
            nonlocal_part = jnp.dot(coefficients, back_ref[x], preferred_element_type=F32)
            beside = both[:, :cells] + nonlocal_part + (read(up) + read(down))
            drift = both[:, cells:] * (a * (scale / (2.0 * SPACING)))
            diag = diag_ref[x][0:1, :] * scale
            kinetic = diag * read(x) - beside * (k2 * scale)
            new = jnp.concatenate([kinetic[half:] - drift[:half], -kinetic[:half] - drift[half:]], axis=0)
            summed = total_ref[x] + new
            total_ref[x] = summed
            if degree < ORDER:
                target[x] = new
                pieces = split(new)
            else:
                pieces = split(summed)
            parts_ref[x] = pieces
            if degree < ORDER:
                overlap = overlap + nt_dot(pieces, fore_ref[x])
            return overlap

        overlap = lax.fori_loop(0, planes, body, jnp.zeros((rows, 4 * nproj), F32))
        source = target

    row_id = lax.broadcasted_iota(jnp.int32, (half, 1), 0)
    occupied = jnp.where(row_id < limit_ref[0], 1.0, 0.0).astype(F32)

    def current(x, acc):
        gradient = jnp.dot(parts_ref[x], stencil_ref[:, cells:], preferred_element_type=F32) * (0.5 / SPACING)
        value = total_ref[x]
        real, imag = value[:half], value[half:]
        if last:
            out_ref[x, :half, :] = real * occupied
            out_ref[x, half:, :] = imag * occupied
        else:
            out_ref[x] = value
        return acc + (
            real * gradient[half:] - imag * gradient[:half] + a * (real * real + imag * imag)
        )

    acc = lax.fori_loop(0, planes, current, jnp.zeros((half, cells), F32))
    total = jnp.sum(acc * occupied) * norm
    current_ref[...] = jnp.full(current_ref.shape, total, F32)


def run_step(field, side, weights, stencil, mix, a, limit, rows, norm, last):
    planes, _, cells = field.shape
    vmem = pl.BlockSpec(memory_space=pltpu.VMEM)
    smem = pl.BlockSpec(memory_space=pltpu.SMEM)
    return pl.pallas_call(
        functools.partial(step_kernel, rows, norm, last),
        out_shape=(
            jax.ShapeDtypeStruct((planes, rows, cells), F32),
            jax.ShapeDtypeStruct((8, 128), F32),
        ),
        in_specs=[smem, smem, vmem, vmem, vmem, vmem, vmem],
        out_specs=(vmem, vmem),
        scratch_shapes=[
            pltpu.VMEM((planes, rows, cells), F32),
            pltpu.VMEM((planes, rows, cells), F32),
            pltpu.VMEM((planes, rows, cells), F32),
            pltpu.VMEM((planes, rows, 2 * cells), BF16),
            pltpu.VMEM((planes, mix.shape[0], cells), BF16),
            pltpu.VMEM((planes, mix.shape[0], 2 * cells), BF16),
            pltpu.VMEM((planes, 8, cells), F32),
        ],
        compiler_params=pltpu.CompilerParams(vmem_limit_bytes=40 * 1024 * 1024),
        name="propagate",
    )(a.reshape(1), limit.reshape(1), field, side, weights, stencil, mix)


def local(
    orbitals, local_potential, projectors, strengths, material, proj_kind, point_cell,
    vector_now, vector_old, devices, grid,
):
    _, points, orb, mine, cells = orbitals.shape
    assert grid % points == 0 and orb % (grid // points) == 0
    share = grid // points
    own = orb // share
    rows = 2 * own
    nproj = projectors.shape[1]
    micro_index, grid_index = lax.axis_index("micro"), lax.axis_index("grid")
    first_point = micro_index * points
    me = first_point + grid_index // share
    first_orbital = (grid_index % share) * own
    kinds = lax.dynamic_slice_in_dim(proj_kind, first_point, points)
    pick = lambda array: lax.dynamic_index_in_dim(array, me, 0, keepdims=False)
    repeat = lambda array: jnp.repeat(array, share, axis=0)
    packed = jnp.concatenate(
        [
            orbitals.reshape(2, points, share, own, mine, cells)
            .transpose(1, 2, 4, 0, 3, 5)
            .reshape(grid, mine, rows, cells),
            repeat(jnp.take(projectors, kinds, axis=0, mode="clip").transpose(0, 2, 1, 3)),
            repeat(jnp.broadcast_to(local_potential[:, :, None, :], (points, mine, 8, cells))),
        ],
        axis=2,
    )
    packed = lax.all_to_all(packed, "grid", split_axis=0, concat_axis=0, tiled=True)
    packed = packed.reshape(grid * mine, -1, cells)
    field, side = packed, packed[:, rows:]
    my_weights = strengths[pick(proj_kind)] * (-2.0 * SPACING**2)
    weights = jnp.broadcast_to(
        jnp.concatenate([my_weights] * 3 + [jnp.zeros_like(my_weights)])[None], (8, 4 * nproj)
    )
    i = lax.broadcasted_iota(jnp.int32, (4 * nproj, 4 * nproj), 0)
    j = lax.broadcasted_iota(jnp.int32, (4 * nproj, 4 * nproj), 1)
    mix = ((i < 2 * nproj) & (i % nproj == j % nproj)).astype(F32)
    stencil = stencil_matrix(cells)
    my_material = pick(material)
    my_cell = pick(point_cell)
    limit = jnp.where(my_material == 1, orb, orb // 2) - first_orbital
    macro_ids = jnp.arange(vector_now.shape[0], dtype=jnp.int32)
    placement = (repeat(point_cell)[:, None] == macro_ids[None, :]).astype(F32)
    present, previous = vector_now, vector_old
    for step in range(STEPS):
        a = lax.dynamic_index_in_dim(present, my_cell, 0, keepdims=False)
        field, current = run_step(
            field, side, weights, stencil, mix, a, limit, rows, 2.0 / (orb * grid * mine * cells), step == STEPS - 1
        )
        spread = jnp.broadcast_to(current[None, :1, :], (devices, 1, 128))
        currents = lax.all_to_all(spread, ("micro", "grid"), split_axis=0, concat_axis=0, tiled=True)[:, 0, 0]
        deposit = jnp.dot(currents, placement, precision=HIGHEST)
        extended = jnp.pad(present, 1)
        curvature = extended[2:] + extended[:-2] - 2.0 * present
        following = 2.0 * present - previous + COURANT**2 * curvature - COUPLING * deposit
        previous, present = present, following
    field = lax.all_to_all(
        field.reshape(grid, mine, rows, cells), "grid", split_axis=0, concat_axis=0, tiled=True
    )
    field = field.reshape(points, share, mine, 2, own, cells).transpose(3, 0, 1, 4, 2, 5)
    field = field.reshape(2, points, orb, mine, cells)
    return field, present


def solution(mesh):
    in_specs = (
        P(None, "micro", None, "grid", None),
        P("micro", "grid", None),
        P(None, None, "grid", None),
        P(),
        P(),
        P(),
        P(),
        P(),
        P(),
    )
    out_specs = (P(None, "micro", None, "grid", None), P())
    body = functools.partial(local, devices=mesh.size, grid=mesh.shape["grid"])
    return jax.shard_map(body, mesh=mesh, in_specs=in_specs, out_specs=out_specs, check_vma=False)
```

```python
import functools

import jax
import jax.numpy as jnp
from jax import lax
from jax.experimental import pallas as pl
from jax.experimental.pallas import tpu as pltpu
from jax.sharding import PartitionSpec as P

NZ = 16
STEPS = 2
ORDER = 4
BLOCK = 8
SMALL = 4

SPACING = 0.64
TIME_STEP = 0.05
COURANT = 0.9
COUPLING = 1.0
HIGHEST = lax.Precision.HIGHEST
F32 = jnp.float32
BF16 = jnp.bfloat16


def split(value):
    high = value.astype(BF16)
    low = (value - high.astype(F32)).astype(BF16)
    return jnp.concatenate([high, low], axis=-1)


def stencil_matrix(cells):
    row = lax.broadcasted_iota(jnp.int32, (cells, cells), 0)
    col = lax.broadcasted_iota(jnp.int32, (cells, cells), 1)
    z = col % NZ
    forward = row == (col - z + (z + 1) % NZ)
    backward = row == (col - z + (z + NZ - 1) % NZ)
    y_next = row == (col + NZ) % cells
    y_last = row == (col + cells - NZ) % cells
    one = lambda m: m.astype(F32)
    beside = one(forward) + one(backward) + one(y_next) + one(y_last)
    both = jnp.concatenate([beside, one(forward) - one(backward)], axis=1)
    return jnp.concatenate([both, both], axis=0).astype(BF16)


def nt_dot(left, right):
    return lax.dot_general(left, right, (((1,), (1,)), ((), ())), preferred_element_type=F32)


def macro_update(present, previous, deposit, macro):
    high, lanes = present.shape
    lane = lax.broadcasted_iota(jnp.int32, present.shape, 1)
    flat = lax.broadcasted_iota(jnp.int32, present.shape, 0) * lanes + lane
    ahead = pltpu.roll(present, lanes - 1, 1)
    ahead = jnp.where(lane == lanes - 1, pltpu.roll(ahead, high - 1, 0), ahead)
    behind = pltpu.roll(present, 1, 1)
    behind = jnp.where(lane == 0, pltpu.roll(behind, 1, 0), behind)
    curvature = ahead + behind - 2.0 * present
    following = 2.0 * present - previous + COURANT**2 * curvature - COUPLING * deposit
    return jnp.where(flat < macro, following, 0.0)


def kernel(
    rows, norm, macro, grid, devices,
    limit_ref, my_cell_ref, cell_ref, field_ref, weight_ref, stencil_ref, mix_ref, now_ref, old_ref,
    out_ref, vector_ref,
    term_a, term_b, total_ref, parts_ref, back_ref, fore_ref, previous_ref,
    mine_ref, currents_ref, send_sem, recv_sem,
):
    planes, cells = total_ref.shape[0], total_ref.shape[2]
    half = rows // 2
    nproj = mix_ref.shape[0] // 4
    k2 = 1.0 / (2.0 * SPACING**2)
    me = lax.axis_index("micro") * grid + lax.axis_index("grid")
    barrier = pltpu.get_barrier_semaphore()

    def peer(distance):
        other = lax.rem(me + distance, devices)
        return other, (other // grid, lax.rem(other, grid))

    @pl.loop(1, devices)
    def _(distance):
        pl.semaphore_signal(barrier, inc=1, device_id=peer(distance)[1], device_id_type=pl.DeviceIdType.MESH)

    def setup(x, overlap):
        beta = field_ref[x, rows:rows + nproj, :]
        high = beta.astype(BF16).astype(F32)
        low = beta - high
        zero = jnp.zeros_like(high)
        back_ref[x] = jnp.concatenate([high, high, low, zero], axis=0).astype(BF16)
        fore = jnp.concatenate([high, low, zero, zero], axis=0).astype(BF16)
        fore_ref[x] = jnp.concatenate([fore, fore], axis=1)
        value = field_ref[x, :rows, :]
        total_ref[x] = value
        term_b[x] = value
        pieces = split(value)
        parts_ref[x] = pieces
        return overlap + nt_dot(pieces, fore_ref[x])

    none = jnp.zeros((rows, 4 * nproj), F32)
    overlap = lax.fori_loop(0, planes, setup, none, unroll=SMALL)
    lane = lax.broadcasted_iota(jnp.int32, (rows, 4 * nproj), 1)
    middle = (lane >= nproj) & (lane < 2 * nproj)
    row_id = lax.broadcasted_iota(jnp.int32, (half, 1), 0)
    occupied = jnp.where(row_id < limit_ref[0], 1.0, 0.0).astype(F32)
    flat = (
        lax.broadcasted_iota(jnp.int32, now_ref.shape, 0) * now_ref.shape[1]
        + lax.broadcasted_iota(jnp.int32, now_ref.shape, 1)
    )
    vector_ref[...] = now_ref[...]
    previous_ref[...] = old_ref[...]
    pl.semaphore_wait(barrier, devices - 1)

    def advance(step, overlap):
        a = jnp.sum(jnp.where(flat == my_cell_ref[0], vector_ref[...], 0.0))
        source = term_b
        for degree in range(1, ORDER + 1):
            target = term_a if degree % 2 == 1 else term_b
            scale = TIME_STEP / degree
            c = jnp.dot(overlap, mix_ref[...], precision=HIGHEST, preferred_element_type=F32) * weight_ref[0:1, :]
            high = c.astype(BF16).astype(F32)
            coefficients = jnp.where(middle, c - high, high).astype(BF16)
            base = 3.0 / SPACING**2 + 0.5 * a * a

            def body(block, overlap, source=source, target=target, scale=scale, coefficients=coefficients, degree=degree):
                x0 = block * BLOCK
                pieces = parts_ref[pl.ds(x0, BLOCK)].reshape(BLOCK * rows, 2 * cells)
                stencils = jnp.dot(pieces, stencil_ref[...], preferred_element_type=F32)
                for offset in range(BLOCK):
                    x = x0 + offset
                    up = lax.rem(x + 1, planes)
                    down = lax.rem(x + planes - 1, planes)
                    both = stencils[offset * rows:(offset + 1) * rows]
                    nonlocal_part = jnp.dot(coefficients, back_ref[x], preferred_element_type=F32)
                    beside = both[:, :cells] + nonlocal_part + (source[up] + source[down])
                    drift = both[:, cells:] * (a * (scale / (2.0 * SPACING)))
                    diag = (field_ref[x, rows + nproj:rows + nproj + 1, :] + base) * scale
                    kinetic = diag * source[x] - beside * (k2 * scale)
                    new = jnp.concatenate([kinetic[half:] - drift[:half], -kinetic[:half] - drift[half:]], axis=0)
                    summed = total_ref[x] + new
                    total_ref[x] = summed
                    term = new if degree < ORDER else summed
                    target[x] = term
                    pieces = split(term)
                    parts_ref[x] = pieces
                    overlap = overlap + nt_dot(pieces, fore_ref[x])
                return overlap

            overlap = lax.fori_loop(0, planes // BLOCK, body, none)
            source = target

        def current(x, acc):
            gradient = jnp.dot(parts_ref[x], stencil_ref[:, cells:], preferred_element_type=F32) * (0.5 / SPACING)
            value = total_ref[x]
            real, imag = value[:half], value[half:]
            return acc + (
                real * gradient[half:] - imag * gradient[:half] + a * (real * real + imag * imag)
            )

        acc = lax.fori_loop(0, planes, current, jnp.zeros((half, cells), F32), unroll=SMALL)
        mine_ref[step] = jnp.full((1, 128), jnp.sum(acc * occupied) * norm, F32)

        def copy(distance):
            other, device = peer(distance)
            return pltpu.make_async_remote_copy(
                src_ref=mine_ref.at[step],
                dst_ref=currents_ref.at[step, me],
                send_sem=send_sem.at[step, distance],
                recv_sem=recv_sem.at[step, me],
                device_id=device,
                device_id_type=pl.DeviceIdType.MESH,
            )

        @pl.loop(1, devices)
        def _(distance):
            copy(distance).start()

        currents_ref[step, me] = mine_ref[step]

        @pl.loop(1, devices)
        def _(distance):
            copy(distance).wait_send()
            other = peer(distance)[0]
            pltpu.make_async_remote_copy(
                src_ref=mine_ref.at[step],
                dst_ref=currents_ref.at[step, other],
                send_sem=send_sem.at[step, distance],
                recv_sem=recv_sem.at[step, other],
                device_id=peer(distance)[1],
                device_id_type=pl.DeviceIdType.MESH,
            ).wait_recv()

        def add(source, deposit):
            return deposit + jnp.where(flat == cell_ref[source], currents_ref[step, source], 0.0)

        deposit = lax.fori_loop(0, devices, add, jnp.zeros(flat.shape, F32), unroll=SMALL)
        present = vector_ref[...]
        vector_ref[...] = macro_update(present, previous_ref[...], deposit, macro)
        previous_ref[...] = present
        return overlap

    lax.fori_loop(0, STEPS, advance, overlap)

    def finish(x, carry):
        value = total_ref[x]
        out_ref[x, :half, :] = value[:half] * occupied
        out_ref[x, half:, :] = value[half:] * occupied
        return carry

    lax.fori_loop(0, planes, finish, 0, unroll=SMALL)


def propagate(limit, my_cell, owners, field, weights, stencil, mix, now, old, rows, norm, macro, grid, devices):
    planes, _, cells = field.shape
    vmem = pl.BlockSpec(memory_space=pltpu.VMEM)
    smem = pl.BlockSpec(memory_space=pltpu.SMEM)
    return pl.pallas_call(
        functools.partial(kernel, rows, norm, macro, grid, devices),
        out_shape=(
            jax.ShapeDtypeStruct((planes, rows, cells), F32),
            jax.ShapeDtypeStruct(now.shape, F32),
        ),
        in_specs=[smem] * 3 + [vmem] * 6,
        out_specs=(vmem, vmem),
        scratch_shapes=[
            pltpu.VMEM((planes, rows, cells), F32),
            pltpu.VMEM((planes, rows, cells), F32),
            pltpu.VMEM((planes, rows, cells), F32),
            pltpu.VMEM((planes, rows, 2 * cells), BF16),
            pltpu.VMEM((planes, mix.shape[0], cells), BF16),
            pltpu.VMEM((planes, mix.shape[0], 2 * cells), BF16),
            pltpu.VMEM(now.shape, F32),
            pltpu.VMEM((STEPS, 1, 128), F32),
            pltpu.VMEM((STEPS, devices, 1, 128), F32),
            pltpu.SemaphoreType.DMA((STEPS, devices)),
            pltpu.SemaphoreType.DMA((STEPS, devices)),
        ],
        compiler_params=pltpu.CompilerParams(
            vmem_limit_bytes=40 * 1024 * 1024, collective_id=0, has_side_effects=True
        ),
        name="propagate",
    )(limit.reshape(1), my_cell.reshape(1), owners, field, weights, stencil, mix, now, old)


def local(
    orbitals, local_potential, projectors, strengths, material, proj_kind, point_cell,
    vector_now, vector_old, devices, grid,
):
    _, points, orb, mine, cells = orbitals.shape
    assert grid % points == 0 and orb % (grid // points) == 0
    share = grid // points
    own = orb // share
    rows = 2 * own
    nproj = projectors.shape[1]
    micro_index, grid_index = lax.axis_index("micro"), lax.axis_index("grid")
    first_point = micro_index * points
    me = first_point + grid_index // share
    first_orbital = (grid_index % share) * own
    kinds = lax.dynamic_slice_in_dim(proj_kind, first_point, points)
    pick = lambda array: lax.dynamic_index_in_dim(array, me, 0, keepdims=False)
    repeat = lambda array: jnp.repeat(array, share, axis=0)
    packed = jnp.concatenate(
        [
            orbitals.reshape(2, points, share, own, mine, cells)
            .transpose(1, 2, 4, 0, 3, 5)
            .reshape(grid, mine, rows, cells),
            repeat(jnp.take(projectors, kinds, axis=0, mode="clip").transpose(0, 2, 1, 3)),
            repeat(jnp.broadcast_to(local_potential[:, :, None, :], (points, mine, 8, cells))),
        ],
        axis=2,
    )
    packed = lax.all_to_all(packed, "grid", split_axis=0, concat_axis=0, tiled=True)
    packed = packed.reshape(grid * mine, -1, cells)
    my_weights = strengths[pick(proj_kind)] * (-2.0 * SPACING**2)
    weights = jnp.broadcast_to(
        jnp.concatenate([my_weights] * 3 + [jnp.zeros_like(my_weights)])[None], (8, 4 * nproj)
    )
    i = lax.broadcasted_iota(jnp.int32, (4 * nproj, 4 * nproj), 0)
    j = lax.broadcasted_iota(jnp.int32, (4 * nproj, 4 * nproj), 1)
    mix = ((i < 2 * nproj) & (i % nproj == j % nproj)).astype(F32)
    stencil = stencil_matrix(cells)
    my_material = pick(material)
    my_cell = pick(point_cell)
    limit = jnp.where(my_material == 1, orb, orb // 2) - first_orbital
    macro = vector_now.shape[0]
    wide = (macro // 1024 + 1) * 1024
    lay = lambda vector: jnp.pad(vector, (0, wide - macro)).reshape(-1, 128)
    field, vector = propagate(
        limit, my_cell, repeat(point_cell), packed, weights, stencil, mix, lay(vector_now), lay(vector_old),
        rows, 2.0 / (orb * grid * mine * cells), macro, grid, devices,
    )
    field = lax.all_to_all(
        field.reshape(grid, mine, rows, cells), "grid", split_axis=0, concat_axis=0, tiled=True
    )
    field = field.reshape(points, share, mine, 2, own, cells).transpose(3, 0, 1, 4, 2, 5)
    field = field.reshape(2, points, orb, mine, cells)
    return field, vector.reshape(-1)[:macro]


def solution(mesh):
    in_specs = (
        P(None, "micro", None, "grid", None),
        P("micro", "grid", None),
        P(None, None, "grid", None),
        P(),
        P(),
        P(),
        P(),
        P(),
        P(),
    )
    out_specs = (P(None, "micro", None, "grid", None), P())
    body = functools.partial(local, devices=mesh.size, grid=mesh.shape["grid"])
    return jax.shard_map(body, mesh=mesh, in_specs=in_specs, out_specs=out_specs, check_vma=False)
```

```python
import functools

import jax
import jax.numpy as jnp
from jax import lax
from jax.experimental import pallas as pl
from jax.experimental.pallas import tpu as pltpu
from jax.sharding import PartitionSpec as P

NZ = 16
STEPS = 2
ORDER = 4
BLOCK = 8
SMALL = 4
GROUPS = 1

SPACING = 0.64
TIME_STEP = 0.05
COURANT = 0.9
COUPLING = 1.0
HIGHEST = lax.Precision.HIGHEST
F32 = jnp.float32
BF16 = jnp.bfloat16


def split(value):
    high = value.astype(BF16)
    low = (value - high.astype(F32)).astype(BF16)
    return jnp.concatenate([high, low], axis=-1)


def stencil_matrix(cells):
    row = lax.broadcasted_iota(jnp.int32, (cells, cells), 0)
    col = lax.broadcasted_iota(jnp.int32, (cells, cells), 1)
    z = col % NZ
    forward = row == (col - z + (z + 1) % NZ)
    backward = row == (col - z + (z + NZ - 1) % NZ)
    y_next = row == (col + NZ) % cells
    y_last = row == (col + cells - NZ) % cells
    one = lambda m: m.astype(F32)
    beside = one(forward) + one(backward) + one(y_next) + one(y_last)
    both = jnp.concatenate([beside, one(forward) - one(backward)], axis=1)
    return jnp.concatenate([both, both], axis=0).astype(BF16)


def nt_dot(left, right):
    return lax.dot_general(left, right, (((1,), (1,)), ((), ())), preferred_element_type=F32)


def macro_update(present, previous, deposit, macro):
    high, lanes = present.shape
    lane = lax.broadcasted_iota(jnp.int32, present.shape, 1)
    flat = lax.broadcasted_iota(jnp.int32, present.shape, 0) * lanes + lane
    ahead = pltpu.roll(present, lanes - 1, 1)
    ahead = jnp.where(lane == lanes - 1, pltpu.roll(ahead, high - 1, 0), ahead)
    behind = pltpu.roll(present, 1, 1)
    behind = jnp.where(lane == 0, pltpu.roll(behind, 1, 0), behind)
    curvature = ahead + behind - 2.0 * present
    following = 2.0 * present - previous + COURANT**2 * curvature - COUPLING * deposit
    return jnp.where(flat < macro, following, 0.0)


def kernel(
    norm, macro, grid, devices,
    limit_ref, my_cell_ref, cell_ref, packed_ref, packed_side_ref, weight_ref, stencil_ref, mix_ref, now_ref, old_ref,
    out_ref, vector_ref,
    total_ref, side_ref, term_a, term_b, parts_ref, back_ref, fore_ref, overlap_ref, previous_ref,
    mine_ref, currents_ref, send_sem, recv_sem,
    in_send, in_recv, side_send, side_recv, out_send, out_recv, own_sem,
):
    groups, planes, rows, cells = total_ref.shape
    mine = planes // grid
    half = rows // 2
    nproj = mix_ref.shape[0] // 4
    k2 = 1.0 / (2.0 * SPACING**2)
    here = lax.axis_index("grid")
    layer = lax.axis_index("micro")
    me = layer * grid + here
    barrier = pltpu.get_barrier_semaphore()

    def peer(distance):
        other = lax.rem(me + distance, devices)
        return other, (other // grid, lax.rem(other, grid))

    def beside_me(distance):
        return lax.rem(here + distance, grid)

    def remote(source, target, sent, received, device):
        return pltpu.make_async_remote_copy(
            src_ref=source, dst_ref=target, send_sem=sent, recv_sem=received,
            device_id=device, device_id_type=pl.DeviceIdType.MESH,
        )

    def planes_of(owner):
        return pl.ds(owner * mine, mine)

    def side_copy(distance, owner):
        other = beside_me(distance)
        return remote(
            packed_side_ref.at[other], side_ref.at[planes_of(owner)],
            side_send.at[distance], side_recv.at[owner], (layer, other),
        )

    def in_copy(group, distance, owner):
        other = beside_me(distance)
        return remote(
            packed_ref.at[group, other], total_ref.at[group, planes_of(owner)],
            in_send.at[group, distance], in_recv.at[group, owner], (layer, other),
        )

    def out_copy(group, distance, owner):
        other = beside_me(distance)
        return remote(
            total_ref.at[group, planes_of(other)], out_ref.at[group, owner],
            out_send.at[group, distance], out_recv.at[group, owner], (layer, other),
        )

    def own_side():
        return pltpu.make_async_copy(packed_side_ref.at[here], side_ref.at[planes_of(here)], own_sem.at[0])

    def own_in(group):
        return pltpu.make_async_copy(
            packed_ref.at[group, here], total_ref.at[group, planes_of(here)], own_sem.at[1 + group]
        )

    def own_out(group):
        return pltpu.make_async_copy(
            total_ref.at[group, planes_of(here)], out_ref.at[group, here], own_sem.at[1 + groups + group]
        )

    @pl.loop(1, devices)
    def _(distance):
        pl.semaphore_signal(barrier, inc=1, device_id=peer(distance)[1], device_id_type=pl.DeviceIdType.MESH)

    own_side().start()
    for group in range(groups):
        own_in(group).start()
    vector_ref[...] = now_ref[...]
    previous_ref[...] = old_ref[...]
    pl.semaphore_wait(barrier, devices - 1)

    @pl.loop(1, grid)
    def _(distance):
        side_copy(distance, here).start()

    for group in range(groups):
        @pl.loop(1, grid)
        def _(distance):
            in_copy(group, distance, here).start()

    own_side().wait()

    @pl.loop(1, grid)
    def _(distance):
        side_copy(distance, here).wait_send()
        side_copy(distance, beside_me(distance)).wait_recv()

    def prepare(x, carry):
        beta = side_ref[x, :nproj, :]
        high = beta.astype(BF16).astype(F32)
        low = beta - high
        zero = jnp.zeros_like(high)
        back_ref[x] = jnp.concatenate([high, high, low, zero], axis=0).astype(BF16)
        fore = jnp.concatenate([high, low, zero, zero], axis=0).astype(BF16)
        fore_ref[x] = jnp.concatenate([fore, fore], axis=1)
        return carry

    lax.fori_loop(0, planes, prepare, 0, unroll=SMALL)
    none = jnp.zeros((rows, 4 * nproj), F32)
    lane = lax.broadcasted_iota(jnp.int32, (rows, 4 * nproj), 1)
    middle = (lane >= nproj) & (lane < 2 * nproj)
    row_id = lax.broadcasted_iota(jnp.int32, (half, 1), 0)
    flat = (
        lax.broadcasted_iota(jnp.int32, now_ref.shape, 0) * now_ref.shape[1]
        + lax.broadcasted_iota(jnp.int32, now_ref.shape, 1)
    )

    def advance_group(step, group, a):
        occupied = jnp.where(row_id + group * half < limit_ref[0], 1.0, 0.0).astype(F32)

        @pl.when(step == 0)
        def _():
            own_in(group).wait()

            @pl.loop(1, grid)
            def _(distance):
                in_copy(group, distance, here).wait_send()
                in_copy(group, distance, beside_me(distance)).wait_recv()

            def setup(x, overlap):
                value = total_ref[group, x]
                term_b[group, x] = value
                pieces = split(value)
                parts_ref[group, x] = pieces
                return overlap + nt_dot(pieces, fore_ref[x])

            overlap_ref[group] = lax.fori_loop(0, planes, setup, none, unroll=SMALL)

        overlap = overlap_ref[group]
        source = term_b
        for degree in range(1, ORDER + 1):
            target = term_a if degree % 2 == 1 else term_b
            scale = TIME_STEP / degree
            c = jnp.dot(overlap, mix_ref[...], precision=HIGHEST, preferred_element_type=F32) * weight_ref[0:1, :]
            high = c.astype(BF16).astype(F32)
            coefficients = jnp.where(middle, c - high, high).astype(BF16)
            base = 3.0 / SPACING**2 + 0.5 * a * a

            def body(block, overlap, source=source, target=target, scale=scale, coefficients=coefficients, degree=degree):
                x0 = block * BLOCK
                pieces = parts_ref[group, pl.ds(x0, BLOCK)].reshape(BLOCK * rows, 2 * cells)
                stencils = jnp.dot(pieces, stencil_ref[...], preferred_element_type=F32)
                for offset in range(BLOCK):
                    x = x0 + offset
                    up = lax.rem(x + 1, planes)
                    down = lax.rem(x + planes - 1, planes)
                    both = stencils[offset * rows:(offset + 1) * rows]
                    nonlocal_part = jnp.dot(coefficients, back_ref[x], preferred_element_type=F32)
                    beside = both[:, :cells] + nonlocal_part + (source[group, up] + source[group, down])
                    drift = both[:, cells:] * (a * (scale / (2.0 * SPACING)))
                    diag = (side_ref[x, nproj:nproj + 1, :] + base) * scale
                    kinetic = diag * source[group, x] - beside * (k2 * scale)
                    new = jnp.concatenate([kinetic[half:] - drift[:half], -kinetic[:half] - drift[half:]], axis=0)
                    summed = total_ref[group, x] + new
                    total_ref[group, x] = summed
                    term = new if degree < ORDER else summed
                    target[group, x] = term
                    pieces = split(term)
                    parts_ref[group, x] = pieces
                    overlap = overlap + nt_dot(pieces, fore_ref[x])
                return overlap

            overlap = lax.fori_loop(0, planes // BLOCK, body, none)
            source = target
        overlap_ref[group] = overlap

        @pl.when(step == STEPS - 1)
        def _():
            def mask(x, carry):
                total_ref[group, x, :half, :] = total_ref[group, x, :half, :] * occupied
                total_ref[group, x, half:, :] = total_ref[group, x, half:, :] * occupied
                return carry

            lax.fori_loop(0, planes, mask, 0, unroll=SMALL)

            @pl.loop(1, grid)
            def _(distance):
                out_copy(group, distance, here).start()

            own_out(group).start()

        def current(x, acc):
            gradient = jnp.dot(parts_ref[group, x], stencil_ref[:, cells:], preferred_element_type=F32) * (0.5 / SPACING)
            value = term_b[group, x]
            real, imag = value[:half], value[half:]
            return acc + (
                real * gradient[half:] - imag * gradient[:half] + a * (real * real + imag * imag)
            )

        acc = lax.fori_loop(0, planes, current, jnp.zeros((half, cells), F32), unroll=SMALL)
        return jnp.sum(acc * occupied, axis=0, keepdims=True)

    def copy(step, distance, owner):
        return remote(
            mine_ref.at[step], currents_ref.at[step, owner],
            send_sem.at[step, distance], recv_sem.at[step, owner], peer(distance)[1],
        )

    def advance(step, carry):
        a = jnp.sum(jnp.where(flat == my_cell_ref[0], vector_ref[...], 0.0))
        acc = advance_group(step, 0, a)
        for group in range(1, groups):
            acc = acc + advance_group(step, group, a)
        mine_ref[step] = jnp.full((1, 128), jnp.sum(acc) * norm, F32)

        @pl.loop(1, devices)
        def _(distance):
            copy(step, distance, me).start()

        currents_ref[step, me] = mine_ref[step]

        @pl.loop(1, devices)
        def _(distance):
            copy(step, distance, me).wait_send()
            copy(step, distance, peer(distance)[0]).wait_recv()

        def add(source, deposit):
            return deposit + jnp.where(flat == cell_ref[source], currents_ref[step, source], 0.0)

        deposit = lax.fori_loop(0, devices, add, jnp.zeros(flat.shape, F32), unroll=SMALL)
        present = vector_ref[...]
        vector_ref[...] = macro_update(present, previous_ref[...], deposit, macro)
        previous_ref[...] = present
        return carry

    lax.fori_loop(0, STEPS, advance, 0)
    for group in range(groups):
        own_out(group).wait()

        @pl.loop(1, grid)
        def _(distance):
            out_copy(group, distance, here).wait_send()
            out_copy(group, distance, beside_me(distance)).wait_recv()


def propagate(limit, my_cell, owners, packed, side, weights, stencil, mix, now, old, norm, macro, grid, devices):
    groups, _, mine, rows, cells = packed.shape
    planes = grid * mine
    assert planes % BLOCK == 0
    vmem = pl.BlockSpec(memory_space=pltpu.VMEM)
    smem = pl.BlockSpec(memory_space=pltpu.SMEM)
    anywhere = pl.BlockSpec(memory_space=pl.ANY)
    return pl.pallas_call(
        functools.partial(kernel, norm, macro, grid, devices),
        out_shape=(
            jax.ShapeDtypeStruct(packed.shape, F32),
            jax.ShapeDtypeStruct(now.shape, F32),
        ),
        in_specs=[smem] * 3 + [anywhere] * 2 + [vmem] * 5,
        out_specs=(anywhere, vmem),
        scratch_shapes=[
            pltpu.VMEM((groups, planes, rows, cells), F32),
            pltpu.VMEM((planes,) + side.shape[2:], F32),
            pltpu.VMEM((groups, planes, rows, cells), F32),
            pltpu.VMEM((groups, planes, rows, cells), F32),
            pltpu.VMEM((groups, planes, rows, 2 * cells), BF16),
            pltpu.VMEM((planes, mix.shape[0], cells), BF16),
            pltpu.VMEM((planes, mix.shape[0], 2 * cells), BF16),
            pltpu.VMEM((groups, rows, mix.shape[0]), F32),
            pltpu.VMEM(now.shape, F32),
            pltpu.VMEM((STEPS, 1, 128), F32),
            pltpu.VMEM((STEPS, devices, 1, 128), F32),
            pltpu.SemaphoreType.DMA((STEPS, devices)),
            pltpu.SemaphoreType.DMA((STEPS, devices)),
            pltpu.SemaphoreType.DMA((groups, grid)),
            pltpu.SemaphoreType.DMA((groups, grid)),
            pltpu.SemaphoreType.DMA((grid,)),
            pltpu.SemaphoreType.DMA((grid,)),
            pltpu.SemaphoreType.DMA((groups, grid)),
            pltpu.SemaphoreType.DMA((groups, grid)),
            pltpu.SemaphoreType.DMA((1 + 2 * groups,)),
        ],
        compiler_params=pltpu.CompilerParams(
            vmem_limit_bytes=48 * 1024 * 1024, collective_id=0, has_side_effects=True
        ),
        name="propagate",
    )(limit.reshape(1), my_cell.reshape(1), owners, packed, side, weights, stencil, mix, now, old)


def local(
    orbitals, local_potential, projectors, strengths, material, proj_kind, point_cell,
    vector_now, vector_old, devices, grid,
):
    _, points, orb, mine, cells = orbitals.shape
    assert grid % points == 0 and orb % (grid // points) == 0
    share = grid // points
    own = orb // share
    nproj = projectors.shape[1]
    micro_index, grid_index = lax.axis_index("micro"), lax.axis_index("grid")
    first_point = micro_index * points
    me = first_point + grid_index // share
    first_orbital = (grid_index % share) * own
    kinds = lax.dynamic_slice_in_dim(proj_kind, first_point, points)
    pick = lambda array: lax.dynamic_index_in_dim(array, me, 0, keepdims=False)
    repeat = lambda array: jnp.repeat(array, share, axis=0)
    packed = (
        orbitals.reshape(2, points, share, GROUPS, own // GROUPS, mine, cells)
        .transpose(3, 1, 2, 5, 0, 4, 6)
        .reshape(GROUPS, grid, mine, 2 * own // GROUPS, cells)
    )
    side = repeat(
        jnp.concatenate(
            [
                jnp.take(projectors, kinds, axis=0, mode="clip").transpose(0, 2, 1, 3),
                jnp.broadcast_to(local_potential[:, :, None, :], (points, mine, 8, cells)),
            ],
            axis=2,
        )
    )
    my_weights = strengths[pick(proj_kind)] * (-2.0 * SPACING**2)
    weights = jnp.broadcast_to(
        jnp.concatenate([my_weights] * 3 + [jnp.zeros_like(my_weights)])[None], (8, 4 * nproj)
    )
    i = lax.broadcasted_iota(jnp.int32, (4 * nproj, 4 * nproj), 0)
    j = lax.broadcasted_iota(jnp.int32, (4 * nproj, 4 * nproj), 1)
    mix = ((i < 2 * nproj) & (i % nproj == j % nproj)).astype(F32)
    stencil = stencil_matrix(cells)
    my_material = pick(material)
    my_cell = pick(point_cell)
    limit = jnp.where(my_material == 1, orb, orb // 2) - first_orbital
    macro = vector_now.shape[0]
    wide = (macro // 1024 + 1) * 1024
    lay = lambda vector: jnp.pad(vector, (0, wide - macro)).reshape(-1, 128)
    field, vector = propagate(
        limit, my_cell, repeat(point_cell), packed, side, weights, stencil, mix, lay(vector_now), lay(vector_old),
        2.0 / (orb * grid * mine * cells), macro, grid, devices,
    )
    field = field.reshape(GROUPS, points, share, mine, 2, own // GROUPS, cells).transpose(4, 1, 2, 0, 5, 3, 6)
    field = field.reshape(2, points, orb, mine, cells)
    return field, vector.reshape(-1)[:macro]


def solution(mesh):
    in_specs = (
        P(None, "micro", None, "grid", None),
        P("micro", "grid", None),
        P(None, None, "grid", None),
        P(),
        P(),
        P(),
        P(),
        P(),
        P(),
    )
    out_specs = (P(None, "micro", None, "grid", None), P())
    body = functools.partial(local, devices=mesh.size, grid=mesh.shape["grid"])
    return jax.shard_map(body, mesh=mesh, in_specs=in_specs, out_specs=out_specs, check_vma=False)
```

```python
import functools

import jax
import jax.numpy as jnp
from jax import lax
from jax.experimental import pallas as pl
from jax.experimental.pallas import tpu as pltpu
from jax.sharding import PartitionSpec as P

NZ = 16
STEPS = 2
ORDER = 4
BLOCK = 8
SMALL = 4
GROUPS = 1

SPACING = 0.64
TIME_STEP = 0.05
COURANT = 0.9
COUPLING = 1.0
HIGHEST = lax.Precision.HIGHEST
F32 = jnp.float32
BF16 = jnp.bfloat16


def split(value):
    high = value.astype(BF16)
    low = (value - high.astype(F32)).astype(BF16)
    return jnp.concatenate([high, low], axis=-1)


def stencil_matrix(cells):
    row = lax.broadcasted_iota(jnp.int32, (cells, cells), 0)
    col = lax.broadcasted_iota(jnp.int32, (cells, cells), 1)
    z = col % NZ
    forward = row == (col - z + (z + 1) % NZ)
    backward = row == (col - z + (z + NZ - 1) % NZ)
    y_next = row == (col + NZ) % cells
    y_last = row == (col + cells - NZ) % cells
    one = lambda m: m.astype(F32)
    beside = one(forward) + one(backward) + one(y_next) + one(y_last)
    both = jnp.concatenate([beside, one(forward) - one(backward)], axis=1)
    return jnp.concatenate([both, both], axis=0).astype(BF16)


def nt_dot(left, right):
    return lax.dot_general(left, right, (((1,), (1,)), ((), ())), preferred_element_type=F32)


def macro_update(present, previous, deposit, macro):
    high, lanes = present.shape
    lane = lax.broadcasted_iota(jnp.int32, present.shape, 1)
    flat = lax.broadcasted_iota(jnp.int32, present.shape, 0) * lanes + lane
    ahead = pltpu.roll(present, lanes - 1, 1)
    ahead = jnp.where(lane == lanes - 1, pltpu.roll(ahead, high - 1, 0), ahead)
    behind = pltpu.roll(present, 1, 1)
    behind = jnp.where(lane == 0, pltpu.roll(behind, 1, 0), behind)
    curvature = ahead + behind - 2.0 * present
    following = 2.0 * present - previous + COURANT**2 * curvature - COUPLING * deposit
    return jnp.where(flat < macro, following, 0.0)


def kernel(
    norm, macro, share, grid, devices,
    material_ref, kind_ref, cell_ref, packed_ref, packed_side_ref, weight_ref, stencil_ref, mix_ref, now_ref, old_ref,
    out_ref, vector_ref,
    total_ref, side_ref, term_a, term_b, parts_ref, back_ref, fore_ref, overlap_ref, previous_ref,
    mine_ref, currents_ref, send_sem, recv_sem,
    in_send, in_recv, side_send, side_recv, out_send, out_recv, own_sem,
):
    groups, planes, rows, cells = total_ref.shape
    mine = planes // grid
    half = rows // 2
    nproj = mix_ref.shape[0] // 4
    k2 = 1.0 / (2.0 * SPACING**2)
    here = lax.axis_index("grid")
    layer = lax.axis_index("micro")
    me = layer * grid + here
    own = groups * half
    first_orbital = lax.rem(here, share) * own
    limit = jnp.where(material_ref[me] == 1, share * own, share * own // 2) - first_orbital
    my_cell, my_kind = cell_ref[me], kind_ref[me]
    weight = jnp.where(my_kind == 0, weight_ref[0:1, :], 0.0)
    for kind in range(1, weight_ref.shape[0]):
        weight = weight + jnp.where(my_kind == kind, weight_ref[kind:kind + 1, :], 0.0)
    barrier = pltpu.get_barrier_semaphore()

    def peer(distance):
        other = lax.rem(me + distance, devices)
        return other, (other // grid, lax.rem(other, grid))

    def beside_me(distance):
        return lax.rem(here + distance, grid)

    def remote(source, target, sent, received, device):
        return pltpu.make_async_remote_copy(
            src_ref=source, dst_ref=target, send_sem=sent, recv_sem=received,
            device_id=device, device_id_type=pl.DeviceIdType.MESH,
        )

    def planes_of(owner):
        return pl.ds(owner * mine, mine)

    def side_copy(distance, owner):
        other = beside_me(distance)
        return remote(
            packed_side_ref.at[other], side_ref.at[planes_of(owner)],
            side_send.at[distance], side_recv.at[owner], (layer, other),
        )

    def in_copy(group, distance, owner):
        other = beside_me(distance)
        return remote(
            packed_ref.at[group, other], total_ref.at[group, planes_of(owner)],
            in_send.at[group, distance], in_recv.at[group, owner], (layer, other),
        )

    def out_copy(group, distance, owner):
        other = beside_me(distance)
        return remote(
            total_ref.at[group, planes_of(other)], out_ref.at[group, owner],
            out_send.at[group, distance], out_recv.at[group, owner], (layer, other),
        )

    def own_side():
        return pltpu.make_async_copy(packed_side_ref.at[here], side_ref.at[planes_of(here)], own_sem.at[0])

    def own_in(group):
        return pltpu.make_async_copy(
            packed_ref.at[group, here], total_ref.at[group, planes_of(here)], own_sem.at[1 + group]
        )

    def own_out(group):
        return pltpu.make_async_copy(
            total_ref.at[group, planes_of(here)], out_ref.at[group, here], own_sem.at[1 + groups + group]
        )

    @pl.loop(1, devices)
    def _(distance):
        pl.semaphore_signal(barrier, inc=1, device_id=peer(distance)[1], device_id_type=pl.DeviceIdType.MESH)

    own_side().start()
    for group in range(groups):
        own_in(group).start()
    vector_ref[...] = now_ref[...]
    previous_ref[...] = old_ref[...]
    pl.semaphore_wait(barrier, devices - 1)

    @pl.loop(1, grid)
    def _(distance):
        side_copy(distance, here).start()

    for group in range(groups):
        @pl.loop(1, grid)
        def _(distance):
            in_copy(group, distance, here).start()

    own_side().wait()

    @pl.loop(1, grid)
    def _(distance):
        side_copy(distance, here).wait_send()
        side_copy(distance, beside_me(distance)).wait_recv()

    def prepare(x, carry):
        beta = side_ref[x, :nproj, :]
        high = beta.astype(BF16).astype(F32)
        low = beta - high
        zero = jnp.zeros_like(high)
        back_ref[x] = jnp.concatenate([high, high, low, zero], axis=0).astype(BF16)
        fore = jnp.concatenate([high, low, zero, zero], axis=0).astype(BF16)
        fore_ref[x] = jnp.concatenate([fore, fore], axis=1)
        return carry

    lax.fori_loop(0, planes, prepare, 0, unroll=SMALL)
    none = jnp.zeros((rows, 4 * nproj), F32)
    lane = lax.broadcasted_iota(jnp.int32, (rows, 4 * nproj), 1)
    middle = (lane >= nproj) & (lane < 2 * nproj)
    row_id = lax.broadcasted_iota(jnp.int32, (half, 1), 0)
    flat = (
        lax.broadcasted_iota(jnp.int32, now_ref.shape, 0) * now_ref.shape[1]
        + lax.broadcasted_iota(jnp.int32, now_ref.shape, 1)
    )

    def advance_group(step, group, a):
        occupied = jnp.where(row_id + group * half < limit, 1.0, 0.0).astype(F32)

        @pl.when(step == 0)
        def _():
            own_in(group).wait()

            @pl.loop(1, grid)
            def _(distance):
                in_copy(group, distance, here).wait_send()
                in_copy(group, distance, beside_me(distance)).wait_recv()

            def setup(x, overlap):
                value = total_ref[group, x]
                term_b[group, x] = value
                pieces = split(value)
                parts_ref[group, x] = pieces
                return overlap + nt_dot(pieces, fore_ref[x])

            overlap_ref[group] = lax.fori_loop(0, planes, setup, none, unroll=SMALL)

        overlap = overlap_ref[group]
        source = term_b
        for degree in range(1, ORDER + 1):
            target = term_a if degree % 2 == 1 else term_b
            scale = TIME_STEP / degree
            c = jnp.dot(overlap, mix_ref[...], precision=HIGHEST, preferred_element_type=F32) * weight
            high = c.astype(BF16).astype(F32)
            coefficients = jnp.where(middle, c - high, high).astype(BF16)
            base = 3.0 / SPACING**2 + 0.5 * a * a

            def body(block, overlap, source=source, target=target, scale=scale, coefficients=coefficients, degree=degree):
                x0 = block * BLOCK
                pieces = parts_ref[group, pl.ds(x0, BLOCK)].reshape(BLOCK * rows, 2 * cells)
                stencils = jnp.dot(pieces, stencil_ref[...], preferred_element_type=F32)
                for offset in range(BLOCK):
                    x = x0 + offset
                    up = lax.rem(x + 1, planes)
                    down = lax.rem(x + planes - 1, planes)
                    both = stencils[offset * rows:(offset + 1) * rows]
                    nonlocal_part = jnp.dot(coefficients, back_ref[x], preferred_element_type=F32)
                    beside = both[:, :cells] + nonlocal_part + (source[group, up] + source[group, down])
                    drift = both[:, cells:] * (a * (scale / (2.0 * SPACING)))
                    diag = (side_ref[x, nproj:nproj + 1, :] + base) * scale
                    kinetic = diag * source[group, x] - beside * (k2 * scale)
                    new = jnp.concatenate([kinetic[half:] - drift[:half], -kinetic[:half] - drift[half:]], axis=0)
                    summed = total_ref[group, x] + new
                    total_ref[group, x] = summed
                    term = new if degree < ORDER else summed
                    target[group, x] = term
                    pieces = split(term)
                    parts_ref[group, x] = pieces
                    overlap = overlap + nt_dot(pieces, fore_ref[x])
                return overlap

            overlap = lax.fori_loop(0, planes // BLOCK, body, none)
            source = target
        overlap_ref[group] = overlap

        @pl.when(step == STEPS - 1)
        def _():
            def mask(x, carry):
                total_ref[group, x, :half, :] = total_ref[group, x, :half, :] * occupied
                total_ref[group, x, half:, :] = total_ref[group, x, half:, :] * occupied
                return carry

            lax.fori_loop(0, planes, mask, 0, unroll=SMALL)

            @pl.loop(1, grid)
            def _(distance):
                out_copy(group, distance, here).start()

            own_out(group).start()

        def current(x, acc):
            gradient = jnp.dot(parts_ref[group, x], stencil_ref[:, cells:], preferred_element_type=F32) * (0.5 / SPACING)
            value = term_b[group, x]
            real, imag = value[:half], value[half:]
            return acc + (
                real * gradient[half:] - imag * gradient[:half] + a * (real * real + imag * imag)
            )

        acc = lax.fori_loop(0, planes, current, jnp.zeros((half, cells), F32), unroll=SMALL)
        return jnp.sum(acc * occupied, axis=0, keepdims=True)

    def copy(step, distance, owner):
        return remote(
            mine_ref.at[step], currents_ref.at[step, owner],
            send_sem.at[step, distance], recv_sem.at[step, owner], peer(distance)[1],
        )

    def advance(step, carry):
        a = jnp.sum(jnp.where(flat == my_cell, vector_ref[...], 0.0))
        acc = advance_group(step, 0, a)
        for group in range(1, groups):
            acc = acc + advance_group(step, group, a)
        mine_ref[step] = jnp.full((1, 128), jnp.sum(acc) * norm, F32)

        @pl.loop(1, devices)
        def _(distance):
            copy(step, distance, me).start()

        currents_ref[step, me] = mine_ref[step]

        @pl.loop(1, devices)
        def _(distance):
            copy(step, distance, me).wait_send()
            copy(step, distance, peer(distance)[0]).wait_recv()

        def add(source, deposit):
            return deposit + jnp.where(flat == cell_ref[source], currents_ref[step, source], 0.0)

        deposit = lax.fori_loop(0, devices, add, jnp.zeros(flat.shape, F32), unroll=SMALL)
        present = vector_ref[...]
        vector_ref[...] = macro_update(present, previous_ref[...], deposit, macro)
        previous_ref[...] = present
        return carry

    lax.fori_loop(0, STEPS, advance, 0)
    for group in range(groups):
        own_out(group).wait()

        @pl.loop(1, grid)
        def _(distance):
            out_copy(group, distance, here).wait_send()
            out_copy(group, distance, beside_me(distance)).wait_recv()


def propagate(materials, kinds, owners, packed, side, weights, stencil, mix, now, old, norm, macro, share, grid, devices):
    groups, _, mine, rows, cells = packed.shape
    planes = grid * mine
    assert planes % BLOCK == 0
    vmem = pl.BlockSpec(memory_space=pltpu.VMEM)
    smem = pl.BlockSpec(memory_space=pltpu.SMEM)
    anywhere = pl.BlockSpec(memory_space=pl.ANY)
    return pl.pallas_call(
        functools.partial(kernel, norm, macro, share, grid, devices),
        out_shape=(
            jax.ShapeDtypeStruct(packed.shape, F32),
            jax.ShapeDtypeStruct(now.shape, F32),
        ),
        in_specs=[smem] * 3 + [anywhere] * 2 + [vmem] * 5,
        out_specs=(anywhere, vmem),
        scratch_shapes=[
            pltpu.VMEM((groups, planes, rows, cells), F32),
            pltpu.VMEM((planes,) + side.shape[2:], F32),
            pltpu.VMEM((groups, planes, rows, cells), F32),
            pltpu.VMEM((groups, planes, rows, cells), F32),
            pltpu.VMEM((groups, planes, rows, 2 * cells), BF16),
            pltpu.VMEM((planes, mix.shape[0], cells), BF16),
            pltpu.VMEM((planes, mix.shape[0], 2 * cells), BF16),
            pltpu.VMEM((groups, rows, mix.shape[0]), F32),
            pltpu.VMEM(now.shape, F32),
            pltpu.VMEM((STEPS, 1, 128), F32),
            pltpu.VMEM((STEPS, devices, 1, 128), F32),
            pltpu.SemaphoreType.DMA((STEPS, devices)),
            pltpu.SemaphoreType.DMA((STEPS, devices)),
            pltpu.SemaphoreType.DMA((groups, grid)),
            pltpu.SemaphoreType.DMA((groups, grid)),
            pltpu.SemaphoreType.DMA((grid,)),
            pltpu.SemaphoreType.DMA((grid,)),
            pltpu.SemaphoreType.DMA((groups, grid)),
            pltpu.SemaphoreType.DMA((groups, grid)),
            pltpu.SemaphoreType.DMA((1 + 2 * groups,)),
        ],
        compiler_params=pltpu.CompilerParams(
            vmem_limit_bytes=48 * 1024 * 1024, collective_id=0, has_side_effects=True
        ),
        name="propagate",
    )(materials, kinds, owners, packed, side, weights, stencil, mix, now, old)


def local(
    orbitals, local_potential, projectors, strengths, material, proj_kind, point_cell,
    vector_now, vector_old, devices, grid,
):
    _, points, orb, mine, cells = orbitals.shape
    assert grid % points == 0 and orb % (grid // points) == 0
    share = grid // points
    own = orb // share
    nproj = projectors.shape[1]
    first_point = lax.axis_index("micro") * points
    kinds = lax.dynamic_slice_in_dim(proj_kind, first_point, points)
    repeat = lambda array: jnp.repeat(array, share, axis=0)
    packed = (
        orbitals.reshape(2, points, share, GROUPS, own // GROUPS, mine, cells)
        .transpose(3, 1, 2, 5, 0, 4, 6)
        .reshape(GROUPS, grid, mine, 2 * own // GROUPS, cells)
    )
    side = repeat(
        jnp.concatenate(
            [
                jnp.take(projectors, kinds, axis=0, mode="clip").transpose(0, 2, 1, 3),
                jnp.broadcast_to(local_potential[:, :, None, :], (points, mine, 8, cells)),
            ],
            axis=2,
        )
    )
    scaled = strengths * (-2.0 * SPACING**2)
    weights = jnp.concatenate([scaled] * 3 + [jnp.zeros_like(scaled)], axis=1)
    i = lax.broadcasted_iota(jnp.int32, (4 * nproj, 4 * nproj), 0)
    j = lax.broadcasted_iota(jnp.int32, (4 * nproj, 4 * nproj), 1)
    mix = ((i < 2 * nproj) & (i % nproj == j % nproj)).astype(F32)
    stencil = stencil_matrix(cells)
    macro = vector_now.shape[0]
    wide = (macro // 1024 + 1) * 1024
    lay = lambda vector: jnp.pad(vector, (0, wide - macro)).reshape(-1, 128)
    field, vector = propagate(
        repeat(material), repeat(proj_kind), repeat(point_cell), packed, side, weights, stencil, mix, lay(vector_now), lay(vector_old),
        2.0 / (orb * grid * mine * cells), macro, share, grid, devices,
    )
    field = field.reshape(GROUPS, points, share, mine, 2, own // GROUPS, cells).transpose(4, 1, 2, 0, 5, 3, 6)
    field = field.reshape(2, points, orb, mine, cells)
    return field, vector.reshape(-1)[:macro]


def solution(mesh):
    in_specs = (
        P(None, "micro", None, "grid", None),
        P("micro", "grid", None),
        P(None, None, "grid", None),
        P(),
        P(),
        P(),
        P(),
        P(),
        P(),
    )
    out_specs = (P(None, "micro", None, "grid", None), P())
    body = functools.partial(local, devices=mesh.size, grid=mesh.shape["grid"])
    return jax.shard_map(body, mesh=mesh, in_specs=in_specs, out_specs=out_specs, check_vma=False)
```
